32 devices in a mesh: groups: 2 (over y), seq: 16 (over z, x, core).
Axes of the slice: x: 2, y: 2, z: 4, core: 2. Of those that a mesh axis runs over, the one named last changes fastest.
Arguments:
- bases: int32 [8192], P(('groups', 'seq')), parts along dimension 0, may hold values from 0 to 3
- base_table: bfloat16 [4, 768], replicated, may hold values from -4 to 4
- first_kernel: bfloat16 [768, 864], P('seq'), may hold values from -0.21875 to 0.21875
- second_kernel: bfloat16 [768, 864], P('seq'), may hold values from -0.21875 to 0.21875
- cotangent: bfloat16 [8192, 768], P(('groups', 'seq')), parts along dimension 0, may hold values from -0.125 to 0.125
Outputs:
- combined: bfloat16 [8192, 768], P(('groups', 'seq')), parts along dimension 0
- first_grad: float32 [1536, 864], P(('groups', 'seq')), parts along dimension 0
- second_grad: float32 [1536, 864], P(('groups', 'seq')), parts along dimension 0
The draws below stay inside these ranges and needn't reach their ends.
There are 2 independent parts, one for each index of `groups`. The reference program is written for one: setup_inputs(seed, part) draws one part's arguments, and reference() takes and returns one part's arrays. A program takes and returns all parts, laid end to end along the dimension named above; an argument that names none is the same for every part. Nothing has to cross between parts.
Inputs may be any that keep to these rules, and one draw needn't show every extreme that they name: `bases`: base codes; the complement of code b is 3 - b.
All inputs are finite; a program needn't handle non-finite values.
Results may differ from the reference program's by a relative error of at most 0.0044.
Values may be sent and summed in bfloat16 or wider, within the bound.
A program may use at most 128 MiB of HBM per device.

```python
import math
import jax
import jax.numpy as jnp
from jax import lax

D = 768
GROUPS = 8
TAPS = 9
CG = 96
LENGTH = 4096


def with_ends(array, key, low, largest):
    index_at = [jax.random.randint(jax.random.fold_in(key, axis), (), 0, length) for axis, length in enumerate(array.shape)]
    longest = array.shape.index(max(array.shape))
    neighbour = index_at[:longest] + [(index_at[longest] + 1) % array.shape[longest]] + index_at[longest + 1:]
    return array.at[tuple(index_at)].set(low).at[tuple(neighbour)].set(largest)


def strengthened(drawn, rng, source, target, shards_of, factor):
    owner, partner = [(jnp.arange(drawn.shape[position]) // (drawn.shape[position] // shards_of)).reshape([-1 if axis == position else 1 for axis in range(drawn.ndim)]) for position in (source, target)]
    chosen = jax.random.permutation(rng, shards_of)[partner]
    strong = (owner == chosen) | (owner == (partner + shards_of // 2) % shards_of)
    return jnp.where(strong, factor * drawn, drawn)


def block_scale(rng, shape, cuts, least, top_value):
    gain, own = 1.0, jax.random.fold_in(rng, 6)
    for axis_at, blocks in cuts:
        draws = jnp.exp(jax.random.uniform(jax.random.fold_in(own, axis_at), (blocks,), jnp.float32, least / len(cuts), top_value / len(cuts)))
        gain = gain * jnp.repeat(draws, shape[axis_at] // blocks).reshape([-1 if axis == axis_at else 1 for axis in range(len(shape))])
    return gain


def scatter_about(key, shape, scale, bound, cuts=(), kind=jnp.bfloat16):
    array = scale * jax.random.normal(key, shape, jnp.float32)
    if cuts:
        array = array * block_scale(key, shape, cuts, -0.22, 0.18)
    return jnp.clip(array, -bound, bound).astype(kind)


def bell_draw_with(key, shape, spread, reach, split, heavy, kind=jnp.bfloat16):
    drawn = spread * jax.random.normal(key, shape, jnp.float32)
    if split:
        drawn = drawn * block_scale(key, shape, split, -0.22, 0.18)
    return jnp.clip(strengthened(drawn, jax.random.fold_in(key, 3), *heavy), -reach, reach).astype(kind)


def setup_inputs(seed: int = 0, part: int = 0) -> dict:
    splits = jax.random.split(jax.random.key(seed), 6)
    part_splits = jax.random.split(jax.random.fold_in(splits[5], part), 6)
    return {
        "bases": with_ends(jax.random.randint(part_splits[0], (LENGTH,), 0, 4), jax.random.fold_in(part_splits[0], 1), 0, 3).astype(jnp.int32),
        "base_table": scatter_about(splits[1], (4, D), 1.0, 4.0),
        "first_kernel": scatter_about(splits[2], (D, TAPS * CG), (TAPS * CG) ** -0.5, 0.21875, ((0, 16),)),
        "second_kernel": scatter_about(splits[3], (D, TAPS * CG), (TAPS * CG) ** -0.5, 0.21875, ((0, 16),)),
        "cotangent": bell_draw_with(part_splits[4], (LENGTH, D), LENGTH ** -0.5, 0.125, ((0, 16),), (0, 1, 16, 2.0)),
    }


def gelu_exact(values):
    return jax.nn.gelu(values, approximate=False)

def to_taps(kernel):
    return jnp.transpose(kernel.reshape(GROUPS, CG, TAPS, CG), (2, 0, 1, 3))

def from_taps(taps):
    return jnp.transpose(taps, (1, 2, 0, 3)).reshape(D, TAPS * CG)

def adjoint(taps):
    return jnp.swapaxes(taps[::-1], 2, 3)

def block_size():
    return math.gcd(LENGTH, 4096)

def convolve(values, taps):
    half_taps = TAPS // 2
    block_rows = block_size()
    padded = jnp.pad(values, ((half_taps, half_taps), (0, 0))).reshape(-1, GROUPS, CG)
    taps_wide = taps.astype(jnp.float32)

    def one_block(offset):
        window = lax.dynamic_slice_in_dim(padded, offset, block_rows + 2 * half_taps, 0).astype(jnp.float32)
        summed = jnp.zeros((block_rows, GROUPS, CG), jnp.float32)
        for tap_index in range(TAPS):
            summed = summed + jnp.einsum('pgc,goc->pgo', window[tap_index:tap_index + block_rows], taps_wide[tap_index])
        return summed
    offsets = jnp.arange(LENGTH // block_rows, dtype=jnp.int32) * block_rows
    return lax.map(one_block, offsets).reshape(LENGTH, D)

def correlate(grad_rows, values):
    half_taps = TAPS // 2
    block_rows = block_size()
    padded = jnp.pad(values, ((half_taps, half_taps), (0, 0))).reshape(-1, GROUPS, CG)
    grad_groups = grad_rows.reshape(-1, GROUPS, CG)

    def accumulate(summed, offset):
        window = lax.dynamic_slice_in_dim(padded, offset, block_rows + 2 * half_taps, 0).astype(jnp.float32)
        grad_part = lax.dynamic_slice_in_dim(grad_groups, offset, block_rows, 0).astype(jnp.float32)
        terms = jnp.stack([jnp.einsum('pgo,pgc->goc', grad_part, window[tap_index:tap_index + block_rows]) for tap_index in range(TAPS)])
        return (summed + terms, None)
    offsets = jnp.arange(LENGTH // block_rows, dtype=jnp.int32) * block_rows
    summed, _ = lax.scan(accumulate, jnp.zeros((TAPS, GROUPS, CG, CG), jnp.float32), offsets)
    return summed

def strand_pass(inputs, first_taps, second_taps, grad_out):
    pre_act = convolve(inputs, first_taps)
    hidden = gelu_exact(pre_act).astype(jnp.bfloat16)
    strand_out = inputs.astype(jnp.float32) + convolve(hidden, second_taps)
    hidden_grad = convolve(grad_out, adjoint(second_taps))
    _, pullback = jax.vjp(gelu_exact, pre_act)
    pre_grad = pullback(hidden_grad)[0].astype(jnp.bfloat16)
    return (strand_out, correlate(pre_grad, inputs), correlate(grad_out, hidden))

def reference(bases, base_table, first_kernel, second_kernel, cotangent):
    first_taps = to_taps(first_kernel)
    second_taps = to_taps(second_kernel)
    forward_in = base_table[bases]
    reverse_in = base_table[3 - bases[::-1]]
    out_forward, first_f, second_f = strand_pass(forward_in, first_taps, second_taps, cotangent)
    out_reverse, first_r, second_r = strand_pass(reverse_in, first_taps, second_taps, cotangent[::-1])
    rounded = lax.optimization_barrier(out_reverse.astype(jnp.bfloat16))
    combined = (out_forward + rounded.astype(jnp.float32)[::-1]).astype(jnp.bfloat16)
    return (combined, from_taps(first_f + first_r), from_taps(second_f + second_r))
```

```python
import functools
import math

import jax
import jax.numpy as jnp
from jax import lax
from jax.experimental import pallas as pl
from jax.experimental.pallas import tpu as pltpu
from jax.sharding import PartitionSpec as P

GROUPS = 8
TAPS = 9
HALF = TAPS // 2
LANES = 128
HIGH = 128
MESH = pl.DeviceIdType.MESH
F32 = jnp.float32
BF16 = jnp.bfloat16


def lane_contract(left, right):
    return lax.dot_general(left, right, (((1,), (1,)), ((), ())), preferred_element_type=F32)


def split_halves(values, axis):
    high = values.astype(BF16).astype(F32)
    column = lax.broadcasted_iota(jnp.int32, values.shape, axis) & 7
    return jnp.where(column < 4, high, values - high).astype(BF16)


def block_kernel(
    count, members, gathered, step,
    codes_ref, diag_ref, skip_ref, first_ref, second_ref, cot_ref,
    comb_ref, first_out, second_out,
    cot_t, codes_in, codes_left, codes_right, cot_in, cot_left, cot_right,
    first_all, second_all, onehot, hid, slope, unf_f, unf_r, cot_unf, adj,
    s_acc, comb_send, comb_in, s_send, s_in, g_send, g_in,
    send_sems, recv_sems,
):
    me = lax.axis_index("seq")
    group = me // members
    member = me % members
    chunk_of = me // GROUPS
    band_of = me % GROUPS
    band = cot_ref.shape[0]
    chunk = band * GROUPS
    width = chunk + LANES
    cg = cot_t.shape[0] // GROUPS
    rows = cg // members
    started = []

    def push(src, dst, kind, recv, target):
        remote = pltpu.make_async_remote_copy(
            src_ref=src, dst_ref=dst, send_sem=send_sems.at[kind], recv_sem=recv_sems.at[recv],
            device_id={"seq": target}, device_id_type=MESH,
        )

        @pl.when(target != me)
        def _():
            remote.start()

        @pl.when(target == me)
        def _():
            pltpu.make_async_copy(src, dst, recv_sems.at[recv]).start()

        started.append((remote, target, None))

    def arrived(ref, recv):
        pltpu.make_async_copy(ref, ref, recv_sems.at[recv]).wait()

    def push_edges(src_of, left_dst, right_dst, kind, recv_left, recv_right):
        for low, dst, recv, here, there in (
            (True, right_dst, recv_right, (band_of == 0) & (chunk_of > 0), chunk_of - 1),
            (False, left_dst, recv_left, (band_of == GROUPS - 1) & (chunk_of < members - 1), chunk_of + 1),
        ):
            for g in range(GROUPS):
                src = src_of(g, low)
                target = g * members + there
                remote = pltpu.make_async_remote_copy(
                    src_ref=src, dst_ref=dst, send_sem=send_sems.at[kind], recv_sem=recv_sems.at[recv],
                    device_id={"seq": target}, device_id_type=MESH,
                )

                @pl.when(here & (target != me))
                def _():
                    remote.start()

                @pl.when(here & (target == me))
                def _():
                    pltpu.make_async_copy(src, dst, recv_sems.at[recv]).start()

                started.append((remote, target, here))

    def edges_arrived(left, right, recv_left, recv_right):
        @pl.when(member > 0)
        def _():
            arrived(left, recv_left)

        @pl.when(member < members - 1)
        def _():
            arrived(right, recv_right)

    barrier = pltpu.get_barrier_semaphore()
    for k in range(1, count):
        pl.semaphore_signal(barrier, inc=1, device_id={"seq": (me + k) % count}, device_id_type=MESH)
    cot_t[...] = jnp.transpose(cot_ref[...])
    hid[...] = jnp.zeros_like(hid)
    pl.semaphore_wait(barrier, count - 1)

    place = pl.ds(pl.multiple_of(band_of * band, LANES), band)
    for g in range(GROUPS):
        push(codes_ref, codes_in.at[:, place], 0, 0, g * members + chunk_of)
    push_edges(
        lambda g, low: codes_ref.at[:, pl.ds(0 if low else band - LANES, LANES)],
        codes_left, codes_right, 1, 1, 2,
    )
    if gathered:
        first = first_ref[...]
        second = second_ref[...]
    else:
        for k in range(members):
            push(first_ref, first_all.at[member], 2, 3, group * members + k)
        for k in range(members):
            push(second_ref, second_all.at[member], 3, 4, group * members + k)
    for g in range(GROUPS):
        push(cot_t.at[pl.ds(cg * g, cg)], cot_in.at[:, place], 4, 5, g * members + chunk_of)
    push_edges(
        lambda g, low: cot_t.at[pl.ds(cg * g, cg), pl.ds(0 if low else band - LANES, LANES)],
        cot_left, cot_right, 5, 6, 7,
    )

    has_right = (member < members - 1).astype(jnp.int32)
    has_left = (member > 0).astype(jnp.int32)

    def edge_mask(height):
        lane = lax.broadcasted_iota(jnp.int32, (height, LANES), 1)
        return lane < LANES // 2, jnp.where(lane < LANES // 2, has_right, has_left) > 0

    arrived(codes_in, 0)
    edges_arrived(codes_left, codes_right, 1, 2)
    on_right, real = edge_mask(8)
    edge = jnp.where(real, jnp.where(on_right, codes_right[...], codes_left[...]), 4)
    codes = jnp.concatenate([codes_in[...], edge], axis=1)
    want = lax.broadcasted_iota(jnp.int32, (8, width), 0) & 3
    onehot[...] = jnp.concatenate(
        [
            jnp.where(pltpu.roll(codes, (HALF - u) % width, 1) == want, 1.0, 0.0)
            for u in range(TAPS)
        ],
        axis=0,
    ).astype(BF16)

    if not gathered:
        arrived(first_all, 3)
        first = first_all[...].reshape(cg, TAPS * cg)
    mix = jnp.concatenate(
        [split_halves(lane_contract(first, diag_ref[s]), 1) for s in range(2)], axis=0
    )

    def activate(cols):
        pre = jnp.dot(mix, onehot[:, cols], preferred_element_type=F32)
        cdf = 0.5 + 0.5 * lax.erf(pre * math.sqrt(0.5))
        return pre * cdf, cdf + pre * jnp.exp(-0.5 * pre * pre) * (1.0 / math.sqrt(2.0 * math.pi))

    @pl.loop(0, chunk // 256)
    def _(i):
        cols = pl.ds(pl.multiple_of(i * 256, 256), 256)
        hidden, grad = activate(cols)
        hidden = hidden.astype(BF16)
        hid[0:cg, cols] = hidden[:cg]
        hid[HIGH : HIGH + cg, cols] = hidden[cg:]
        slope[:, cols] = grad

    hidden, _ = activate(pl.ds(chunk, LANES))
    _, real = edge_mask(2 * cg)
    hidden = jnp.where(real, hidden, 0.0).astype(BF16)
    hid[0:cg, chunk:] = hidden[:cg]
    hid[HIGH : HIGH + cg, chunk:] = hidden[cg:]

    for t in range(TAPS):
        unf_f[cg * t : cg * (t + 1), :] = pltpu.roll(hid[0:cg, :], (HALF - t) % width, 1)[:, :chunk]
        unf_r[cg * t : cg * (t + 1), :] = pltpu.roll(
            hid[HIGH : HIGH + cg, :], (t - HALF) % width, 1
        )[:, :chunk]

    if not gathered:
        arrived(second_all, 4)
        second = second_all[...].reshape(cg, TAPS * cg)

    @pl.loop(0, chunk // step)
    def _(i):
        cols = pl.ds(pl.multiple_of(i * step, step), step)
        out_f = jnp.dot(second, unf_f[:, cols], preferred_element_type=F32)
        out_f += jnp.dot(skip_ref[0], onehot[:, cols], preferred_element_type=F32)
        out_r = jnp.dot(second, unf_r[:, cols], preferred_element_type=F32)
        out_r += jnp.dot(skip_ref[1], onehot[:, cols], preferred_element_type=F32)
        comb_send[:, cols] = (out_f + out_r.astype(BF16).astype(F32)).astype(BF16)

    for j in range(GROUPS):
        push(comb_send.at[:, pl.ds(j * band, band)], comb_in.at[group], 6, 8, member * GROUPS + j)

    arrived(cot_in, 5)
    edges_arrived(cot_left, cot_right, 6, 7)
    on_right, real = edge_mask(cg)
    edge = jnp.where(
        real, jnp.where(on_right, cot_right[...].astype(F32), cot_left[...].astype(F32)), 0.0
    ).astype(BF16)
    cot = jnp.concatenate([cot_in[...], edge], axis=1)
    for t in range(TAPS):
        cot_unf[cg * t : cg * (t + 1), :] = pltpu.roll(cot, (HALF - t) % width, 1)[:, :chunk]

    s_acc[...] = jnp.zeros_like(s_acc)

    @pl.loop(0, chunk // step)
    def _(i):
        cols = pl.ds(pl.multiple_of(i * step, step), step)
        s_acc[...] += lane_contract(cot_unf[:, cols], hid[:, cols])

    for t in range(TAPS):
        block = (
            s_acc[cg * (TAPS - 1 - t) : cg * (TAPS - t), 0:cg]
            + s_acc[cg * t : cg * (t + 1), HIGH : HIGH + cg]
        )
        if gathered:
            second_out[t] = block
        else:
            for k in range(members):
                s_send[k, t] = block[rows * k : rows * (k + 1)]
    if not gathered:
        for k in range(members):
            push(s_send.at[k], s_in.at[member], 7, 9, group * members + k)

    turned = jnp.transpose(second)
    for u in range(TAPS):
        v = TAPS - 1 - u
        adj[u, 0:cg] = turned[cg * v : cg * (v + 1)]
        adj[u, cg:] = turned[cg * u : cg * (u + 1)]

    def backward(i, total):
        cols = pl.ds(pl.multiple_of(i * step, step), step)
        grad = jnp.dot(adj[0], cot_unf[0:cg, cols], preferred_element_type=F32)
        for u in range(1, TAPS):
            grad += jnp.dot(adj[u], cot_unf[cg * u : cg * (u + 1), cols], preferred_element_type=F32)
        pre_grad = (grad * slope[:, cols]).astype(BF16)
        return total + lane_contract(pre_grad, onehot[:, cols])

    terms = lax.fori_loop(0, chunk // step, backward, jnp.zeros((2 * cg, 8 * TAPS), F32))
    if gathered:
        first_out[0] = terms[:cg]
        first_out[1] = terms[cg:]
    else:
        for k in range(members):
            for s in range(2):
                g_send[k, s] = terms[s * cg + rows * k : s * cg + rows * (k + 1)]
        for k in range(members):
            push(g_send.at[k], g_in.at[member], 8, 10, group * members + k)

    arrived(comb_in, 8)
    comb_ref[...] = jnp.transpose(comb_in[...].reshape(GROUPS * cg, band))
    if not gathered:
        arrived(s_in, 9)
        second_out[...] = jnp.sum(s_in[...], axis=0)
        arrived(g_in, 10)
        summed = jnp.sum(g_in[...], axis=0)
        first_out[...] = jnp.dot(
            split_halves(summed[0], 1), diag_ref[0], preferred_element_type=F32
        ) + jnp.dot(split_halves(summed[1], 1), diag_ref[1], preferred_element_type=F32)

    for remote, target, here in started:
        @pl.when((target != me) if here is None else (here & (target != me)))
        def _():
            remote.wait_send()


def per_device(bases, base_table, first_kernel, second_kernel, cotangent):
    band, channels = cotangent.shape
    cg = channels // GROUPS
    count = lax.axis_size("seq")
    members = count // GROUPS
    rows = first_kernel.shape[0]
    chunk = band * GROUPS
    width = chunk + LANES
    step = math.gcd(chunk, 512)
    me = lax.axis_index("seq")
    gathered = rows % 16 != 0

    table = lax.dynamic_slice_in_dim(base_table, (me // members) * cg, cg, axis=1)
    columns = 8 * TAPS
    offset = jnp.arange(columns) // 8
    high = jnp.arange(columns) % 8 < 4
    tap = jnp.arange(TAPS * cg) // cg
    zero = jnp.zeros((), BF16)
    diag, skip = [], []
    for s in range(2):
        strand = table if s == 0 else table[::-1]
        wanted = offset if s == 0 else TAPS - 1 - offset
        diag.append(jnp.where(wanted[:, None] == tap[None, :], jnp.tile(strand, (2 * TAPS, TAPS)), zero))
        chosen = ((offset == HALF) & high)[None, :]
        skip.append(jnp.where(chosen, jnp.tile(strand.T, (1, 2 * TAPS)), zero))
    diag, skip = jnp.stack(diag), jnp.stack(skip)
    codes = jnp.broadcast_to(bases[None, :], (8, band))

    if gathered:
        same = [[g * members + k for k in range(members)] for g in range(GROUPS)]
        first_kernel = lax.all_gather(first_kernel, "seq", axis=0, tiled=True, axis_index_groups=same)
        second_kernel = lax.all_gather(second_kernel, "seq", axis=0, tiled=True, axis_index_groups=same)
        outs = ((2, cg, columns), (TAPS, cg, cg))
        lot, lot_rows = 1, 16
    else:
        outs = ((rows, TAPS * cg), (TAPS, rows, cg))
        lot, lot_rows = members, rows

    vmem = pltpu.VMEM
    combined, first_grad, second_grad = pl.pallas_call(
        functools.partial(block_kernel, count, members, gathered, step),
        out_shape=(
            jax.ShapeDtypeStruct((band, channels), BF16),
            jax.ShapeDtypeStruct(outs[0], F32),
            jax.ShapeDtypeStruct(outs[1], F32),
        ),
        in_specs=[pl.BlockSpec(memory_space=vmem)] * 6,
        out_specs=[pl.BlockSpec(memory_space=vmem)] * 3,
        scratch_shapes=[
            vmem((channels, band), BF16),
            vmem((8, chunk), jnp.int32),
            vmem((8, LANES), jnp.int32),
            vmem((8, LANES), jnp.int32),
            vmem((cg, chunk), BF16),
            vmem((cg, LANES), BF16),
            vmem((cg, LANES), BF16),
            vmem((lot, lot_rows, TAPS * cg), BF16),
            vmem((lot, lot_rows, TAPS * cg), BF16),
            vmem((columns, width), BF16),
            vmem((2 * HIGH, width), BF16),
            vmem((2 * cg, chunk), F32),
            vmem((TAPS * cg, chunk), BF16),
            vmem((TAPS * cg, chunk), BF16),
            vmem((TAPS * cg, chunk), BF16),
            vmem((TAPS, 2 * cg, cg), BF16),
            vmem((TAPS * cg, 2 * HIGH), F32),
            vmem((cg, chunk), BF16),
            vmem((GROUPS, cg, band), BF16),
            vmem((lot, TAPS, lot_rows, cg), F32),
            vmem((lot, TAPS, lot_rows, cg), F32),
            vmem((lot, 2, lot_rows, columns), F32),
            vmem((lot, 2, lot_rows, columns), F32),
            pltpu.SemaphoreType.DMA((9,)),
            pltpu.SemaphoreType.DMA((11,)),
        ],
        compiler_params=pltpu.CompilerParams(
            collective_id=0, has_side_effects=True, vmem_limit_bytes=56 * 1024 * 1024
        ),
    )(codes, diag, skip, first_kernel, second_kernel, cotangent)

    if gathered:
        first_local = jnp.zeros((cg, TAPS * cg), F32)
        for s in range(2):
            first_local += jnp.einsum(
                "oc,ck->ok",
                jnp.where(high[None, :], first_grad[s], 0.0),
                diag[s].astype(F32),
                precision=lax.Precision.HIGHEST,
            )
        second_local = jnp.transpose(second_grad, (1, 0, 2)).reshape(cg, TAPS * cg)
        scatter = functools.partial(
            lax.psum_scatter, axis_name="seq", scatter_dimension=0, tiled=True, axis_index_groups=same
        )
        return combined, scatter(first_local), scatter(second_local)
    return combined, first_grad, jnp.transpose(second_grad, (1, 0, 2)).reshape(rows, TAPS * cg)


def solution(mesh):
    return jax.shard_map(
        per_device,
        mesh=mesh,
        in_specs=(
            P(("groups", "seq")),
            P(),
            P("seq", None),
            P("seq", None),
            P(("groups", "seq"), None),
        ),
        out_specs=(
            P(("groups", "seq"), None),
            P(("groups", "seq"), None),
            P(("groups", "seq"), None),
        ),
        check_vma=False,
    )
```

```python
import functools
import math

import jax
import jax.numpy as jnp
from jax import lax
from jax.experimental import pallas as pl
from jax.experimental.pallas import tpu as pltpu
from jax.sharding import PartitionSpec as P

GROUPS = 8
TAPS = 9
HALF = TAPS // 2
LANES = 128
HIGH = 128
MESH = pl.DeviceIdType.MESH
F32 = jnp.float32
BF16 = jnp.bfloat16


def lane_contract(left, right):
    return lax.dot_general(left, right, (((1,), (1,)), ((), ())), preferred_element_type=F32)


def split_halves(values, axis):
    high = values.astype(BF16).astype(F32)
    column = lax.broadcasted_iota(jnp.int32, values.shape, axis) & 7
    return jnp.where(column < 4, high, values - high).astype(BF16)


def block_kernel(
    count, members, gathered, step,
    bases_ref, table_ref, first_ref, second_ref, cot_ref,
    comb_in, first_out, second_out, diag_out,
    diag_ref, skip_ref, edges, codes_ref, cot_t, codes_in, codes_left, codes_right, cot_in, cot_left, cot_right,
    first_all, second_all, onehot, hid, slope, unf_f, unf_r, cot_unf, adj,
    s_acc, comb_send, s_send, g_send,
    send_sems, recv_sems, diag_sem,
):
    me = lax.axis_index("seq")
    group = me // members
    member = me % members
    chunk_of = me // GROUPS
    band_of = me % GROUPS
    band = cot_ref.shape[0]
    chunk = band * GROUPS
    width = chunk + LANES
    cg = cot_t.shape[0] // GROUPS
    s_rows = cg if gathered else cg // members
    started = []

    def keep_for_send(src, dst, kind, recv, target):
        remote = pltpu.make_async_remote_copy(
            src_ref=src, dst_ref=dst, send_sem=send_sems.at[kind], recv_sem=recv_sems.at[recv],
            device_id={"seq": target}, device_id_type=MESH,
        )
        started.append((remote, target, None))
        return remote

    def push(src, dst, kind, recv, target, keep=True):
        remote = keep_for_send(src, dst, kind, recv, target)
        if not keep:
            started.pop()

        @pl.when(target != me)
        def _():
            remote.start()

        @pl.when(target == me)
        def _():
            pltpu.make_async_copy(src, dst, recv_sems.at[recv]).start()

    def arrived(ref, recv):
        pltpu.make_async_copy(ref, ref, recv_sems.at[recv]).wait()

    def push_edges(src_of, left_dst, right_dst, kind, recv_left, recv_right):
        for low, dst, recv, here, there in (
            (True, right_dst, recv_right, (band_of == 0) & (chunk_of > 0), chunk_of - 1),
            (False, left_dst, recv_left, (band_of == GROUPS - 1) & (chunk_of < members - 1), chunk_of + 1),
        ):
            for g in range(GROUPS):
                src = src_of(g, low)
                target = g * members + there
                remote = pltpu.make_async_remote_copy(
                    src_ref=src, dst_ref=dst, send_sem=send_sems.at[kind], recv_sem=recv_sems.at[recv],
                    device_id={"seq": target}, device_id_type=MESH,
                )

                @pl.when(here & (target != me))
                def _():
                    remote.start()

                @pl.when(here & (target == me))
                def _():
                    pltpu.make_async_copy(src, dst, recv_sems.at[recv]).start()

                started.append((remote, target, here))

    def edges_arrived(left, right, recv_left, recv_right):
        @pl.when(member > 0)
        def _():
            arrived(left, recv_left)

        @pl.when(member < members - 1)
        def _():
            arrived(right, recv_right)

    barrier = pltpu.get_barrier_semaphore()
    for k in range(1, count):
        pl.semaphore_signal(barrier, inc=1, device_id={"seq": (me + k) % count}, device_id_type=MESH)
    codes_ref[...] = jnp.broadcast_to(bases_ref[...], codes_ref.shape)
    cot_t[...] = jnp.transpose(cot_ref[...])
    for g in range(GROUPS):
        edges[0, g] = cot_ref[0:16, cg * g : cg * (g + 1)]
        edges[1, g] = cot_ref[band - 16 :, cg * g : cg * (g + 1)]
    pl.semaphore_wait(barrier, count - 1)

    place = pl.ds(pl.multiple_of(band_of * band, LANES), band)
    for g in range(GROUPS):
        push(codes_ref, codes_in.at[:, place], 0, 0, g * members + chunk_of)
    push_edges(
        lambda g, low: codes_ref.at[:, pl.ds(0 if low else band - LANES, LANES)],
        codes_left, codes_right, 1, 1, 2,
    )
    if gathered:
        first = first_ref[...]
        second = second_ref[...]
    else:
        for k in range(members):
            push(first_ref, first_all.at[member], 2, 3, group * members + k)
        for k in range(members):
            push(second_ref, second_all.at[member], 3, 4, group * members + k)
    for g in range(GROUPS):
        push(cot_t.at[pl.ds(cg * g, cg)], cot_in.at[:, place], 4, 5, g * members + chunk_of)
    push_edges(lambda g, low: edges.at[0 if low else 1, g], cot_left, cot_right, 5, 6, 7)

    channels = GROUPS * cg
    row = lax.broadcasted_iota(jnp.int32, (16, channels), 0)
    lane = lax.broadcasted_iota(jnp.int32, (16, channels), 1)
    code = jnp.where(row < 8, row & 3, 3 - (row & 3))
    table = table_ref[...].astype(F32)
    wide = jnp.zeros((16, channels), F32)
    for c in range(4):
        wide = jnp.where(code == c, table[c : c + 1], wide)
    wide = jnp.where(lane < cg, pltpu.roll(wide, (channels - group * cg) % channels, 1), 0.0)
    wide = jnp.concatenate([wide, jnp.zeros((16, LANES), F32)], axis=1)
    eye = (
        lax.broadcasted_iota(jnp.int32, (cg, cg), 0) == lax.broadcasted_iota(jnp.int32, (cg, cg), 1)
    ).astype(F32).astype(BF16)
    for s in range(2):
        strand = wide[8 * s : 8 * (s + 1)]
        diag_ref[s] = jnp.concatenate(
            [pltpu.roll(strand, cg * (u if s == 0 else TAPS - 1 - u), 1) for u in range(TAPS)], axis=0
        )[:, : TAPS * cg].astype(BF16)
        own = jnp.where(lax.broadcasted_iota(jnp.int32, (8, cg), 0) < 4, strand[:, :cg], 0.0)
        blank = jnp.zeros((8 * HALF, cg), F32)
        skip_ref[s] = lane_contract(
            eye, jnp.concatenate([blank, own, blank], axis=0).astype(BF16)
        ).astype(BF16)
    pltpu.make_async_copy(diag_ref, diag_out, diag_sem).start()
    for top in (cg, HIGH + cg):
        hid[top : top + HIGH - cg, :] = jnp.zeros((HIGH - cg, width), BF16)

    has_right = (member < members - 1).astype(jnp.int32)
    has_left = (member > 0).astype(jnp.int32)

    def edge_mask(height):
        lane = lax.broadcasted_iota(jnp.int32, (height, LANES), 1)
        return lane < LANES // 2, jnp.where(lane < LANES // 2, has_right, has_left) > 0

    arrived(codes_in, 0)
    edges_arrived(codes_left, codes_right, 1, 2)
    on_right, real = edge_mask(8)
    edge = jnp.where(real, jnp.where(on_right, codes_right[...], codes_left[...]), 4)
    codes = jnp.concatenate([codes_in[...], edge], axis=1)
    want = lax.broadcasted_iota(jnp.int32, (8, width), 0) & 3
    onehot[...] = jnp.concatenate(
        [
            jnp.where(pltpu.roll(codes, (HALF - u) % width, 1) == want, 1.0, 0.0)
            for u in range(TAPS)
        ],
        axis=0,
    ).astype(BF16)

    if not gathered:
        arrived(first_all, 3)
        first = first_all[...].reshape(cg, TAPS * cg)
    mix = jnp.concatenate(
        [split_halves(lane_contract(first, diag_ref[s]), 1) for s in range(2)], axis=0
    )

    def activate(cols):
        pre = jnp.dot(mix, onehot[:, cols], preferred_element_type=F32)
        cdf = 0.5 + 0.5 * lax.erf(pre * math.sqrt(0.5))
        return pre * cdf, cdf + pre * jnp.exp(-0.5 * pre * pre) * (1.0 / math.sqrt(2.0 * math.pi))

    @pl.loop(0, chunk // 256)
    def _(i):
        cols = pl.ds(pl.multiple_of(i * 256, 256), 256)
        hidden, grad = activate(cols)
        hidden = hidden.astype(BF16)
        hid[0:cg, cols] = hidden[:cg]
        hid[HIGH : HIGH + cg, cols] = hidden[cg:]
        slope[:, cols] = grad

    hidden, _ = activate(pl.ds(chunk, LANES))
    _, real = edge_mask(2 * cg)
    hidden = jnp.where(real, hidden, 0.0).astype(BF16)
    hid[0:cg, chunk:] = hidden[:cg]
    hid[HIGH : HIGH + cg, chunk:] = hidden[cg:]

    for t in range(TAPS):
        unf_f[cg * t : cg * (t + 1), :] = pltpu.roll(hid[0:cg, :], (HALF - t) % width, 1)[:, :chunk]
        unf_r[cg * t : cg * (t + 1), :] = pltpu.roll(
            hid[HIGH : HIGH + cg, :], (t - HALF) % width, 1
        )[:, :chunk]

    if not gathered:
        arrived(second_all, 4)
        second = second_all[...].reshape(cg, TAPS * cg)

    @pl.loop(0, chunk // step)
    def _(i):
        cols = pl.ds(pl.multiple_of(i * step, step), step)
        out_f = jnp.dot(second, unf_f[:, cols], preferred_element_type=F32)
        out_f += jnp.dot(skip_ref[0], onehot[:, cols], preferred_element_type=F32)
        out_r = jnp.dot(second, unf_r[:, cols], preferred_element_type=F32)
        out_r += jnp.dot(skip_ref[1], onehot[:, cols], preferred_element_type=F32)
        comb_send[:, cols] = (out_f + out_r.astype(BF16).astype(F32)).astype(BF16)
        for k in range(step // band):
            j = i * (step // band) + k
            push(
                comb_send.at[:, pl.ds(pl.multiple_of(j * band, LANES), band)], comb_in.at[group],
                6, 8, member * GROUPS + j, keep=False,
            )

    for j in range(GROUPS):
        keep_for_send(
            comb_send.at[:, pl.ds(j * band, band)], comb_in.at[group], 6, 8, member * GROUPS + j
        )

    arrived(cot_in, 5)
    edges_arrived(cot_left, cot_right, 6, 7)
    edge = jnp.transpose(
        jnp.concatenate(
            [
                jnp.where(has_right > 0, cot_right[...].astype(F32), 0.0),
                jnp.zeros((LANES - 32, cg), F32),
                jnp.where(has_left > 0, cot_left[...].astype(F32), 0.0),
            ],
            axis=0,
        )
    ).astype(BF16)
    cot = jnp.concatenate([cot_in[...], edge], axis=1)
    for t in range(TAPS):
        cot_unf[cg * t : cg * (t + 1), :] = pltpu.roll(cot, (HALF - t) % width, 1)[:, :chunk]

    s_acc[...] = jnp.zeros_like(s_acc)

    @pl.loop(0, chunk // step)
    def _(i):
        cols = pl.ds(pl.multiple_of(i * step, step), step)
        s_acc[...] += lane_contract(cot_unf[:, cols], hid[:, cols])

    for t in range(TAPS):
        block = (
            s_acc[cg * (TAPS - 1 - t) : cg * (TAPS - t), 0:cg]
            + s_acc[cg * t : cg * (t + 1), HIGH : HIGH + cg]
        )
        for k in range(members if not gathered else 1):
            s_send[k, t] = block[s_rows * k : s_rows * (k + 1)]
    if gathered:
        pltpu.make_async_copy(s_send.at[0], second_out.at[0], recv_sems.at[9]).start()
    else:
        for k in range(members):
            push(s_send.at[k], second_out.at[member], 7, 9, group * members + k)

    turned = jnp.transpose(second)
    for u in range(TAPS):
        v = TAPS - 1 - u
        adj[u, 0:cg] = turned[cg * v : cg * (v + 1)]
        adj[u, cg:] = turned[cg * u : cg * (u + 1)]

    def backward(i, total):
        cols = pl.ds(pl.multiple_of(i * step, step), step)
        grad = jnp.dot(adj[0], cot_unf[0:cg, cols], preferred_element_type=F32)
        for u in range(1, TAPS):
            grad += jnp.dot(adj[u], cot_unf[cg * u : cg * (u + 1), cols], preferred_element_type=F32)
        pre_grad = (grad * slope[:, cols]).astype(BF16)
        return total + lane_contract(pre_grad, onehot[:, cols])

    terms = lax.fori_loop(0, chunk // step, backward, jnp.zeros((2 * cg, 8 * TAPS), F32))
    for k in range(members if not gathered else 1):
        for s in range(2):
            g_send[k, s] = terms[s * cg + s_rows * k : s * cg + s_rows * (k + 1)]
    if gathered:
        pltpu.make_async_copy(g_send.at[0], first_out.at[0], recv_sems.at[10]).start()
    else:
        for k in range(members):
            push(g_send.at[k], first_out.at[member], 8, 10, group * members + k)

    pltpu.make_async_copy(diag_ref, diag_out, diag_sem).wait()
    arrived(comb_in, 8)
    arrived(second_out, 9)
    arrived(first_out, 10)
    for remote, target, here in started:
        @pl.when((target != me) if here is None else (here & (target != me)))
        def _():
            remote.wait_send()


def finish_kernel(comb_in, first_in, second_in, diag_ref, comb_ref, first_ref, second_ref):
    taps, _, cg = second_in.shape[1:]
    comb_ref[...] = jnp.transpose(comb_in[...].reshape(comb_in.shape[0] * cg, comb_in.shape[2]))
    summed = jnp.sum(second_in[...], axis=0)
    for t in range(taps):
        second_ref[:, cg * t : cg * (t + 1)] = summed[t]
    terms = jnp.sum(first_in[...], axis=0)
    first_ref[...] = jnp.dot(
        split_halves(terms[0], 1), diag_ref[0], preferred_element_type=F32
    ) + jnp.dot(split_halves(terms[1], 1), diag_ref[1], preferred_element_type=F32)


def per_device(bases, base_table, first_kernel, second_kernel, cotangent):
    band, channels = cotangent.shape
    cg = channels // GROUPS
    count = lax.axis_size("seq")
    members = count // GROUPS
    rows = first_kernel.shape[0]
    chunk = band * GROUPS
    width = chunk + LANES
    step = math.gcd(chunk, 512)
    gathered = rows % 16 != 0

    columns = 8 * TAPS
    if gathered:
        same = [[g * members + k for k in range(members)] for g in range(GROUPS)]
        first_kernel = lax.all_gather(first_kernel, "seq", axis=0, tiled=True, axis_index_groups=same)
        second_kernel = lax.all_gather(second_kernel, "seq", axis=0, tiled=True, axis_index_groups=same)
        lot, lot_rows = 1, cg
    else:
        lot, lot_rows = members, rows

    vmem = pltpu.VMEM
    comb_parts, first_parts, second_parts, diag = pl.pallas_call(
        functools.partial(block_kernel, count, members, gathered, step),
        out_shape=(
            jax.ShapeDtypeStruct((GROUPS, cg, band), BF16),
            jax.ShapeDtypeStruct((lot, 2, lot_rows, columns), F32),
            jax.ShapeDtypeStruct((lot, TAPS, lot_rows, cg), F32),
            jax.ShapeDtypeStruct((2, columns, TAPS * cg), BF16),
        ),
        in_specs=[pl.BlockSpec(memory_space=vmem)] * 5,
        out_specs=[pl.BlockSpec(memory_space=pl.ANY)] * 4,
        scratch_shapes=[
            vmem((2, columns, TAPS * cg), BF16),
            vmem((2, cg, columns), BF16),
            vmem((2, GROUPS, 16, cg), BF16),
            vmem((8, band), jnp.int32),
            vmem((channels, band), BF16),
            vmem((8, chunk), jnp.int32),
            vmem((8, LANES), jnp.int32),
            vmem((8, LANES), jnp.int32),
            vmem((cg, chunk), BF16),
            vmem((16, cg), BF16),
            vmem((16, cg), BF16),
            vmem((lot, lot_rows, TAPS * cg), BF16),
            vmem((lot, lot_rows, TAPS * cg), BF16),
            vmem((columns, width), BF16),
            vmem((2 * HIGH, width), BF16),
            vmem((2 * cg, chunk), F32),
            vmem((TAPS * cg, chunk), BF16),
            vmem((TAPS * cg, chunk), BF16),
            vmem((TAPS * cg, chunk), BF16),
            vmem((TAPS, 2 * cg, cg), BF16),
            vmem((TAPS * cg, 2 * HIGH), F32),
            vmem((cg, chunk), BF16),
            vmem((lot, TAPS, lot_rows, cg), F32),
            vmem((lot, 2, lot_rows, columns), F32),
            pltpu.SemaphoreType.DMA((9,)),
            pltpu.SemaphoreType.DMA((11,)),
            pltpu.SemaphoreType.DMA,
        ],
        compiler_params=pltpu.CompilerParams(
            collective_id=0, has_side_effects=True, vmem_limit_bytes=56 * 1024 * 1024
        ),
    )(bases.reshape(1, band), base_table, first_kernel, second_kernel, cotangent)

    finished = pl.pallas_call(
        finish_kernel,
        out_shape=(
            jax.ShapeDtypeStruct((band, channels), BF16),
            jax.ShapeDtypeStruct((lot_rows, TAPS * cg), F32),
            jax.ShapeDtypeStruct((lot_rows, TAPS * cg), F32),
        ),
        in_specs=[pl.BlockSpec(memory_space=vmem)] * 4,
        out_specs=[pl.BlockSpec(memory_space=vmem)] * 3,
    )(comb_parts, first_parts, second_parts, diag)
    if gathered:
        scatter = functools.partial(
            lax.psum_scatter, axis_name="seq", scatter_dimension=0, tiled=True, axis_index_groups=same
        )
        return finished[0], scatter(finished[1]), scatter(finished[2])
    return tuple(finished)


def solution(mesh):
    return jax.shard_map(
        per_device,
        mesh=mesh,
        in_specs=(
            P(("groups", "seq")),
            P(),
            P("seq", None),
            P("seq", None),
            P(("groups", "seq"), None),
        ),
        out_specs=(
            P(("groups", "seq"), None),
            P(("groups", "seq"), None),
            P(("groups", "seq"), None),
        ),
        check_vma=False,
    )
```

```python
import functools
import math

import jax
import jax.numpy as jnp
from jax import lax
from jax.experimental import pallas as pl
from jax.experimental.pallas import tpu as pltpu
from jax.sharding import PartitionSpec as P

GROUPS = 8
TAPS = 9
HALF = TAPS // 2
LANES = 128
HIGH = 128
MESH = pl.DeviceIdType.MESH
F32 = jnp.float32
BF16 = jnp.bfloat16


def lane_contract(left, right):
    return lax.dot_general(left, right, (((1,), (1,)), ((), ())), preferred_element_type=F32)


def split_halves(values, axis):
    high = values.astype(BF16).astype(F32)
    column = lax.broadcasted_iota(jnp.int32, values.shape, axis) & 7
    return jnp.where(column < 4, high, values - high).astype(BF16)


def block_kernel(
    count, members, gathered, step,
    bases_ref, table_ref, first_ref, second_ref, cot_ref,
    comb_in, first_out, second_out, diag_out,
    diag_ref, diag_own, skip_ref, edges, codes_ref, cot_t, codes_in, codes_left, codes_right, cot_in, cot_left, cot_right,
    first_all, second_all, onehot, hid, slope, unf_f, unf_r, cot_unf, adj,
    s_acc, comb_send, s_send, g_send,
    send_sems, recv_sems, diag_sem,
):
    me = lax.axis_index("seq")
    group = me % GROUPS
    member = me // GROUPS
    band_of = group
    owned, piece = me // members, me % members
    band = cot_ref.shape[0]
    chunk = band * GROUPS
    width = chunk + LANES
    cg = cot_t.shape[0] // GROUPS
    s_rows = cg if gathered else cg // members
    started = []

    def keep_for_send(src, dst, kind, recv, target):
        remote = pltpu.make_async_remote_copy(
            src_ref=src, dst_ref=dst, send_sem=send_sems.at[kind], recv_sem=recv_sems.at[recv],
            device_id={"seq": target}, device_id_type=MESH,
        )
        started.append((remote, target, None))
        return remote

    def push(src, dst, kind, recv, target, keep=True):
        remote = keep_for_send(src, dst, kind, recv, target)
        if not keep:
            started.pop()

        @pl.when(target != me)
        def _():
            remote.start()

        @pl.when(target == me)
        def _():
            pltpu.make_async_copy(src, dst, recv_sems.at[recv]).start()

    def arrived(ref, recv):
        pltpu.make_async_copy(ref, ref, recv_sems.at[recv]).wait()

    def push_edges(src_of, left_dst, right_dst, kind, recv_left, recv_right):
        for low, dst, recv, here, there in (
            (True, right_dst, recv_right, (band_of == 0) & (member > 0), member - 1),
            (False, left_dst, recv_left, (band_of == GROUPS - 1) & (member < members - 1), member + 1),
        ):
            for g in range(GROUPS):
                src = src_of(g, low)
                target = there * GROUPS + g
                remote = pltpu.make_async_remote_copy(
                    src_ref=src, dst_ref=dst, send_sem=send_sems.at[kind], recv_sem=recv_sems.at[recv],
                    device_id={"seq": target}, device_id_type=MESH,
                )

                @pl.when(here & (target != me))
                def _():
                    remote.start()

                @pl.when(here & (target == me))
                def _():
                    pltpu.make_async_copy(src, dst, recv_sems.at[recv]).start()

                started.append((remote, target, here))

    def edges_arrived(left, right, recv_left, recv_right):
        @pl.when(member > 0)
        def _():
            arrived(left, recv_left)

        @pl.when(member < members - 1)
        def _():
            arrived(right, recv_right)

    barrier = pltpu.get_barrier_semaphore()
    for k in range(1, count):
        pl.semaphore_signal(barrier, inc=1, device_id={"seq": (me + k) % count}, device_id_type=MESH)
    codes_ref[...] = jnp.broadcast_to(bases_ref[...], codes_ref.shape)
    cot_t[...] = jnp.transpose(cot_ref[...])
    for g in range(GROUPS):
        edges[0, g] = cot_ref[0:16, cg * g : cg * (g + 1)]
        edges[1, g] = cot_ref[band - 16 :, cg * g : cg * (g + 1)]
    pl.semaphore_wait(barrier, count - 1)

    place = pl.ds(pl.multiple_of(band_of * band, LANES), band)
    for g in range(GROUPS):
        push(codes_ref, codes_in.at[:, place], 0, 0, member * GROUPS + g)
    push_edges(
        lambda g, low: codes_ref.at[:, pl.ds(0 if low else band - LANES, LANES)],
        codes_left, codes_right, 1, 1, 2,
    )
    if gathered:
        first = first_ref[...]
        second = second_ref[...]
    else:
        for k in range(members):
            push(first_ref, first_all.at[piece], 2, 3, k * GROUPS + owned)
        for k in range(members):
            push(second_ref, second_all.at[piece], 3, 4, k * GROUPS + owned)
    for g in range(GROUPS):
        push(cot_t.at[pl.ds(cg * g, cg)], cot_in.at[:, place], 4, 5, member * GROUPS + g)
    push_edges(lambda g, low: edges.at[0 if low else 1, g], cot_left, cot_right, 5, 6, 7)

    channels = GROUPS * cg

    def group_table(of_group):
        row = lax.broadcasted_iota(jnp.int32, (16, channels), 0)
        lane = lax.broadcasted_iota(jnp.int32, (16, channels), 1)
        code = jnp.where(row < 8, row & 3, 3 - (row & 3))
        table = table_ref[...].astype(F32)
        wide = jnp.zeros((16, channels), F32)
        for c in range(4):
            wide = jnp.where(code == c, table[c : c + 1], wide)
        shift = (channels - of_group * cg) % channels
        wide = jnp.where(lane < cg, pltpu.roll(wide, shift, 1), 0.0)
        return jnp.concatenate([wide, jnp.zeros((16, LANES), F32)], axis=1)

    def spread(strand, s):
        return jnp.concatenate(
            [pltpu.roll(strand, cg * (u if s == 0 else TAPS - 1 - u), 1) for u in range(TAPS)], axis=0
        )[:, : TAPS * cg].astype(BF16)

    wide = group_table(group)
    eye = (
        lax.broadcasted_iota(jnp.int32, (cg, cg), 0) == lax.broadcasted_iota(jnp.int32, (cg, cg), 1)
    ).astype(F32).astype(BF16)
    for s in range(2):
        strand = wide[8 * s : 8 * (s + 1)]
        diag_ref[s] = spread(strand, s)
        own = jnp.where(lax.broadcasted_iota(jnp.int32, (8, cg), 0) < 4, strand[:, :cg], 0.0)
        blank = jnp.zeros((8 * HALF, cg), F32)
        skip_ref[s] = lane_contract(
            eye, jnp.concatenate([blank, own, blank], axis=0).astype(BF16)
        ).astype(BF16)
    for top in (cg, HIGH + cg):
        hid[top : top + HIGH - cg, :] = jnp.zeros((HIGH - cg, width), BF16)

    has_right = (member < members - 1).astype(jnp.int32)
    has_left = (member > 0).astype(jnp.int32)

    def edge_mask(height):
        lane = lax.broadcasted_iota(jnp.int32, (height, LANES), 1)
        return lane < LANES // 2, jnp.where(lane < LANES // 2, has_right, has_left) > 0

    arrived(codes_in, 0)
    edges_arrived(codes_left, codes_right, 1, 2)
    on_right, real = edge_mask(8)
    edge = jnp.where(real, jnp.where(on_right, codes_right[...], codes_left[...]), 4)
    codes = jnp.concatenate([codes_in[...], edge], axis=1)
    want = lax.broadcasted_iota(jnp.int32, (8, width), 0) & 3
    onehot[...] = jnp.concatenate(
        [
            jnp.where(pltpu.roll(codes, (HALF - u) % width, 1) == want, 1.0, 0.0)
            for u in range(TAPS)
        ],
        axis=0,
    ).astype(BF16)

    if not gathered:
        arrived(first_all, 3)
        first = first_all[...].reshape(cg, TAPS * cg)
    mix = jnp.concatenate(
        [split_halves(lane_contract(first, diag_ref[s]), 1) for s in range(2)], axis=0
    )

    def activate(cols):
        pre = jnp.dot(mix, onehot[:, cols], preferred_element_type=F32)
        cdf = 0.5 + 0.5 * lax.erf(pre * math.sqrt(0.5))
        return pre * cdf, cdf + pre * jnp.exp(-0.5 * pre * pre) * (1.0 / math.sqrt(2.0 * math.pi))

    @pl.loop(0, chunk // step)
    def _(i):
        cols = pl.ds(pl.multiple_of(i * step, step), step)
        hidden, grad = activate(cols)
        hidden = hidden.astype(BF16)
        hid[0:cg, cols] = hidden[:cg]
        hid[HIGH : HIGH + cg, cols] = hidden[cg:]
        slope[:, cols] = grad

    hidden, _ = activate(pl.ds(chunk, LANES))
    _, real = edge_mask(2 * cg)
    hidden = jnp.where(real, hidden, 0.0).astype(BF16)
    hid[0:cg, chunk:] = hidden[:cg]
    hid[HIGH : HIGH + cg, chunk:] = hidden[cg:]

    for t in range(TAPS):
        unf_f[cg * t : cg * (t + 1), :] = pltpu.roll(hid[0:cg, :], (HALF - t) % width, 1)[:, :chunk]
        unf_r[cg * t : cg * (t + 1), :] = pltpu.roll(
            hid[HIGH : HIGH + cg, :], (t - HALF) % width, 1
        )[:, :chunk]

    if not gathered:
        arrived(second_all, 4)
        second = second_all[...].reshape(cg, TAPS * cg)

    @pl.loop(0, chunk // step)
    def _(i):
        cols = pl.ds(pl.multiple_of(i * step, step), step)
        out_f = jnp.dot(second, unf_f[:, cols], preferred_element_type=F32)
        out_f += jnp.dot(skip_ref[0], onehot[:, cols], preferred_element_type=F32)
        out_r = jnp.dot(second, unf_r[:, cols], preferred_element_type=F32)
        out_r += jnp.dot(skip_ref[1], onehot[:, cols], preferred_element_type=F32)
        comb_send[:, cols] = (out_f + out_r.astype(BF16).astype(F32)).astype(BF16)
        for k in range(step // band):
            j = i * (step // band) + k
            push(
                comb_send.at[:, pl.ds(pl.multiple_of(j * band, LANES), band)], comb_in.at[group],
                6, 8, member * GROUPS + j, keep=False,
            )

    for j in range(GROUPS):
        keep_for_send(
            comb_send.at[:, pl.ds(j * band, band)], comb_in.at[group], 6, 8, member * GROUPS + j
        )

    arrived(cot_in, 5)
    edges_arrived(cot_left, cot_right, 6, 7)
    edge = jnp.transpose(
        jnp.concatenate(
            [
                jnp.where(has_right > 0, cot_right[...].astype(F32), 0.0),
                jnp.zeros((LANES - 32, cg), F32),
                jnp.where(has_left > 0, cot_left[...].astype(F32), 0.0),
            ],
            axis=0,
        )
    ).astype(BF16)
    cot = jnp.concatenate([cot_in[...], edge], axis=1)
    for t in range(TAPS):
        cot_unf[cg * t : cg * (t + 1), :] = pltpu.roll(cot, (HALF - t) % width, 1)[:, :chunk]

    s_acc[...] = lane_contract(cot_unf[...], hid[:, :chunk])

    for t in range(TAPS):
        block = (
            s_acc[cg * (TAPS - 1 - t) : cg * (TAPS - t), 0:cg]
            + s_acc[cg * t : cg * (t + 1), HIGH : HIGH + cg]
        )
        for k in range(members if not gathered else 1):
            s_send[k, t] = block[s_rows * k : s_rows * (k + 1)]
    if gathered:
        pltpu.make_async_copy(s_send.at[0], second_out.at[0], recv_sems.at[9]).start()
    else:
        for k in range(members):
            push(s_send.at[k], second_out.at[member], 7, 9, group * members + k)

    wide = group_table(group if gathered else owned)
    for s in range(2):
        diag_own[s] = spread(wide[8 * s : 8 * (s + 1)], s)
    pltpu.make_async_copy(diag_own, diag_out, diag_sem).start()

    turned = jnp.transpose(second)
    for u in range(TAPS):
        v = TAPS - 1 - u
        adj[u, 0:cg] = turned[cg * v : cg * (v + 1)]
        adj[u, cg:] = turned[cg * u : cg * (u + 1)]

    grad = jnp.dot(adj[0], cot_unf[0:cg, :], preferred_element_type=F32)
    for u in range(1, TAPS):
        grad += jnp.dot(adj[u], cot_unf[cg * u : cg * (u + 1), :], preferred_element_type=F32)
    terms = lane_contract((grad * slope[...]).astype(BF16), onehot[:, :chunk])
    for k in range(members if not gathered else 1):
        for s in range(2):
            g_send[k, s] = terms[s * cg + s_rows * k : s * cg + s_rows * (k + 1)]
    if gathered:
        pltpu.make_async_copy(g_send.at[0], first_out.at[0], recv_sems.at[10]).start()
    else:
        for k in range(members):
            push(g_send.at[k], first_out.at[member], 8, 10, group * members + k)

    pltpu.make_async_copy(diag_own, diag_out, diag_sem).wait()
    arrived(comb_in, 8)
    arrived(second_out, 9)
    arrived(first_out, 10)
    for remote, target, here in started:
        @pl.when((target != me) if here is None else (here & (target != me)))
        def _():
            remote.wait_send()


def finish_kernel(comb_in, first_in, second_in, diag_ref, comb_ref, first_ref, second_ref):
    taps, _, cg = second_in.shape[1:]
    comb_ref[...] = jnp.transpose(comb_in[...].reshape(comb_in.shape[0] * cg, comb_in.shape[2]))
    summed = jnp.sum(second_in[...], axis=0)
    for t in range(taps):
        second_ref[:, cg * t : cg * (t + 1)] = summed[t]
    terms = jnp.sum(first_in[...], axis=0)
    first_ref[...] = jnp.dot(
        split_halves(terms[0], 1), diag_ref[0], preferred_element_type=F32
    ) + jnp.dot(split_halves(terms[1], 1), diag_ref[1], preferred_element_type=F32)


def per_device(bases, base_table, first_kernel, second_kernel, cotangent):
    band, channels = cotangent.shape
    cg = channels // GROUPS
    count = lax.axis_size("seq")
    members = count // GROUPS
    rows = first_kernel.shape[0]
    chunk = band * GROUPS
    width = chunk + LANES
    step = math.gcd(chunk, 512)
    gathered = rows % 16 != 0

    columns = 8 * TAPS
    if gathered:
        group = lax.axis_index("seq") % GROUPS
        first_kernel, second_kernel = (
            lax.dynamic_slice_in_dim(
                lax.all_gather(kernel, "seq", axis=0, tiled=True), group * cg, cg, axis=0
            )
            for kernel in (first_kernel, second_kernel)
        )
        lot, lot_rows = 1, cg
    else:
        lot, lot_rows = members, rows

    vmem = pltpu.VMEM
    comb_parts, first_parts, second_parts, diag = pl.pallas_call(
        functools.partial(block_kernel, count, members, gathered, step),
        out_shape=(
            jax.ShapeDtypeStruct((GROUPS, cg, band), BF16),
            jax.ShapeDtypeStruct((lot, 2, lot_rows, columns), F32),
            jax.ShapeDtypeStruct((lot, TAPS, lot_rows, cg), F32),
            jax.ShapeDtypeStruct((2, columns, TAPS * cg), BF16),
        ),
        in_specs=[pl.BlockSpec(memory_space=vmem)] * 5,
        out_specs=[pl.BlockSpec(memory_space=pl.ANY)] * 4,
        scratch_shapes=[
            vmem((2, columns, TAPS * cg), BF16),
            vmem((2, columns, TAPS * cg), BF16),
            vmem((2, cg, columns), BF16),
            vmem((2, GROUPS, 16, cg), BF16),
            vmem((8, band), jnp.int32),
            vmem((channels, band), BF16),
            vmem((8, chunk), jnp.int32),
            vmem((8, LANES), jnp.int32),
            vmem((8, LANES), jnp.int32),
            vmem((cg, chunk), BF16),
            vmem((16, cg), BF16),
            vmem((16, cg), BF16),
            vmem((lot, lot_rows, TAPS * cg), BF16),
            vmem((lot, lot_rows, TAPS * cg), BF16),
            vmem((columns, width), BF16),
            vmem((2 * HIGH, width), BF16),
            vmem((2 * cg, chunk), F32),
            vmem((TAPS * cg, chunk), BF16),
            vmem((TAPS * cg, chunk), BF16),
            vmem((TAPS * cg, chunk), BF16),
            vmem((TAPS, 2 * cg, cg), BF16),
            vmem((TAPS * cg, 2 * HIGH), F32),
            vmem((cg, chunk), BF16),
            vmem((lot, TAPS, lot_rows, cg), F32),
            vmem((lot, 2, lot_rows, columns), F32),
            pltpu.SemaphoreType.DMA((9,)),
            pltpu.SemaphoreType.DMA((11,)),
            pltpu.SemaphoreType.DMA,
        ],
        compiler_params=pltpu.CompilerParams(
            collective_id=0, has_side_effects=True, vmem_limit_bytes=56 * 1024 * 1024
        ),
    )(bases.reshape(1, band), base_table, first_kernel, second_kernel, cotangent)

    finished = pl.pallas_call(
        finish_kernel,
        out_shape=(
            jax.ShapeDtypeStruct((band, channels), BF16),
            jax.ShapeDtypeStruct((lot_rows, TAPS * cg), F32),
            jax.ShapeDtypeStruct((lot_rows, TAPS * cg), F32),
        ),
        in_specs=[pl.BlockSpec(memory_space=vmem)] * 4,
        out_specs=[pl.BlockSpec(memory_space=vmem)] * 3,
    )(comb_parts, first_parts, second_parts, diag)
    if gathered:
        blank = jnp.zeros((channels, TAPS * cg), F32)
        first_grad, second_grad = (
            lax.psum_scatter(
                lax.dynamic_update_slice_in_dim(blank, grad, group * cg, axis=0),
                "seq", scatter_dimension=0, tiled=True,
            )
            for grad in finished[1:]
        )
        return finished[0], first_grad, second_grad
    return tuple(finished)


def solution(mesh):
    return jax.shard_map(
        per_device,
        mesh=mesh,
        in_specs=(
            P(("groups", "seq")),
            P(),
            P("seq", None),
            P("seq", None),
            P(("groups", "seq"), None),
        ),
        out_specs=(
            P(("groups", "seq"), None),
            P(("groups", "seq"), None),
            P(("groups", "seq"), None),
        ),
        check_vma=False,
    )
```
